32 devices in a mesh: bucket: 16 (over z, y, core), edge: 2 (over x).
Axes of the slice: x: 2, y: 2, z: 4, core: 2. Of those that a mesh axis runs over, the one named last changes fastest.
Arguments:
- left_slab: bfloat16 [6144, 256], P(('bucket', 'edge')), may hold values from -1.5 to 1.5
- right_slab: bfloat16 [6144, 256], P(('bucket', 'edge')), may hold values from -1.5 to 1.5
- relation: float32 [1024, 256], replicated, may hold values from 0.5 to 1.5
- src_ids: int32 [2, 16, 4096], P(None, 'bucket', 'edge'), may hold values from 0 to 383
- dst_ids: int32 [2, 16, 4096], P(None, 'bucket', 'edge'), may hold values from 0 to 383
- rel_ids: int32 [2, 16, 4096], P(None, 'bucket', 'edge'), may hold values from 0 to 1023
- neg_ids: int32 [2, 16, 16, 512], P(None, 'bucket', 'edge'), may hold values from 0 to 383
- edge_counts: int32 [2, 16], P(None, 'bucket'), may hold values from 1 to 4096, as said below
Outputs:
- left_out: bfloat16 [6144, 256], P(('bucket', 'edge'))
- right_out: bfloat16 [6144, 256], P(('bucket', 'edge'))
- relation_out: float32 [1024, 256], replicated
The draws below stay inside these ranges and needn't reach their ends.
Inputs may be any that keep to these rules, and one draw needn't show every extreme that they name: `edge_counts`: live edges are the first slots of a bucket; in every round some bucket has all 4096 slots live.
All inputs are finite; a program needn't handle non-finite values.
Results may differ from the reference program's by a relative error of at most 0.0046.
Values may be sent and summed in bfloat16 or wider, within the bound.
A program may use at most 64 MiB of HBM per device.

```python
import jax
import jax.numpy as jnp
from jax import lax

W = 256
RELS = 1024
SPAN = 256
NEG = 512
ROUNDS = 2
SPANS_DEV = 8
GROUPS = 16
SLAB = 384
CAP = 4096
N_EDGE = 2


def draw_edge_counts(key, part):
    key_base = jax.random.fold_in(key, 11)
    key_full = jax.random.fold_in(key, 12)
    base = jax.random.randint(key_base, (ROUNDS, GROUPS), CAP // 8, CAP // 2 + 1)
    full = jax.random.randint(key_full, (ROUNDS,), 0, GROUPS)
    chosen = jnp.arange(GROUPS)[None, :] == full[:, None]
    return jnp.where(chosen, CAP, base).astype(jnp.int32)


def touch_ends(array, key, low, top_value):
    shape = array.shape
    index_at = [jax.random.randint(jax.random.fold_in(key, axis), (), 0, shape[axis]) for axis in range(len(shape))]
    array = array.at[tuple(index_at)].set(low)
    longest = shape.index(max(shape))
    index_at[longest] = (index_at[longest] + 1) % shape[longest]
    return array.at[tuple(index_at)].set(top_value)


def block_scale(rng, shape, cuts, smallest, high):
    loudness, own = 1.0, jax.random.fold_in(rng, 6)
    for axis_at, parts in cuts:
        draws = jnp.exp(jax.random.uniform(jax.random.fold_in(own, axis_at), (parts,), jnp.float32, smallest / len(cuts), high / len(cuts)))
        loudness = loudness * jnp.repeat(draws, shape[axis_at] // parts).reshape([-1 if axis == axis_at else 1 for axis in range(len(shape))])
    return loudness


def scatter_about(key, extent, width, most, pieces=(), kind=jnp.bfloat16):
    result = jax.random.normal(key, extent, jnp.float32) * width
    if len(pieces) > 0:
        result = block_scale(key, extent, pieces, -0.22, 0.18) * result
    return jnp.clip(result, min=-most, max=most).astype(kind)


def setup_inputs(seed: int = 0) -> dict:
    arg_keys = jax.random.split(jax.random.key(seed), 9)
    left_slab = scatter_about(arg_keys[0], (GROUPS * SLAB, W), 0.25, 1.5, ((0, 32),))
    right_slab = scatter_about(arg_keys[1], (GROUPS * SLAB, W), 0.25, 1.5, ((0, 32),))
    relation = jnp.clip(jax.random.uniform(arg_keys[2], (RELS, W), jnp.float32, 0.5, 1.5), 0.5, 1.5)
    src_ids = touch_ends(jax.random.randint(arg_keys[3], (ROUNDS, GROUPS, CAP), 0, SLAB), jax.random.fold_in(arg_keys[3], 1), 0, SLAB - 1).astype(jnp.int32)
    dst_ids = touch_ends(jax.random.randint(arg_keys[4], (ROUNDS, GROUPS, CAP), 0, SLAB), jax.random.fold_in(arg_keys[4], 1), 0, SLAB - 1).astype(jnp.int32)
    rel_ids = touch_ends(jax.random.randint(arg_keys[5], (ROUNDS, GROUPS, CAP), 0, RELS), jax.random.fold_in(arg_keys[5], 1), 0, RELS - 1).astype(jnp.int32)
    neg_ids = touch_ends(jax.random.randint(arg_keys[6], (ROUNDS, GROUPS, SPANS_DEV * N_EDGE, NEG), 0, SLAB), jax.random.fold_in(arg_keys[6], 1), 0, SLAB - 1).astype(jnp.int32)
    edge_counts = draw_edge_counts(jax.random.fold_in(arg_keys[8], 71), 0)
    return dict(left_slab=left_slab, right_slab=right_slab, relation=relation, src_ids=src_ids, dst_ids=dst_ids, rel_ids=rel_ids, neg_ids=neg_ids, edge_counts=edge_counts)


learn_rate = 0.05
relation_rate = 0.05


def span_grads(left, right, theta, src_c, dst_c, rel_c, neg_c, mask):
    s_rows = left[src_c]
    d_rows = right[dst_c]
    negatives = right[neg_c]
    t_rows = theta[rel_c]
    s_wide = s_rows.astype(jnp.float32)
    q_rows = (s_wide * t_rows).astype(jnp.bfloat16)
    q_wide = q_rows.astype(jnp.float32)
    d_wide = d_rows.astype(jnp.float32)
    pos = jnp.sum(q_wide * d_wide, axis=-1)
    scores = jnp.dot(q_rows, negatives.T, preferred_element_type=jnp.float32)
    g_pos = -jax.nn.sigmoid(-pos) * mask
    g_neg = (jax.nn.sigmoid(scores) * mask[:, None]).astype(jnp.bfloat16)
    g_q = g_pos[:, None] * d_wide + jnp.dot(g_neg, negatives, preferred_element_type=jnp.float32)
    g_d = g_pos[:, None] * q_wide
    g_negrows = jnp.dot(g_neg.T, q_rows, preferred_element_type=jnp.float32)
    g_s = g_q * t_rows
    g_t = g_q * s_wide
    return g_s, g_d, g_negrows, g_t


def bucket_grads(left, right, theta, src, dst, rel, neg, count):
    n_live = (count + SPAN - 1) // SPAN

    def step(c, carry):
        g_left, g_right, g_theta = carry
        mask = ((c * SPAN + jnp.arange(SPAN)) < count).astype(jnp.float32)
        g_s, g_d, g_negrows, g_t = span_grads(left, right, theta, src[c], dst[c], rel[c], neg[c], mask)
        g_left = g_left.at[src[c]].add(g_s)
        g_right = g_right.at[dst[c]].add(g_d).at[neg[c]].add(g_negrows)
        g_theta = g_theta.at[rel[c]].add(g_t)
        return g_left, g_right, g_theta

    init = (jnp.zeros((SLAB, W), jnp.float32), jnp.zeros((SLAB, W), jnp.float32), jnp.zeros((RELS, W), jnp.float32))
    return lax.fori_loop(0, n_live, step, init)


def reference(left_slab, right_slab, relation, src_ids, dst_ids, rel_ids, neg_ids, edge_counts):
    lefts = left_slab.reshape(GROUPS, SLAB, W)
    rights = right_slab.reshape(GROUPS, SLAB, W)
    theta = relation
    blocks = CAP // SPAN
    for rnd in range(ROUNDS):
        if rnd > 0:
            rights = jnp.roll(rights, 1, axis=0)
        src = src_ids[rnd].reshape(GROUPS, blocks, SPAN)
        dst = dst_ids[rnd].reshape(GROUPS, blocks, SPAN)
        rel = rel_ids[rnd].reshape(GROUPS, blocks, SPAN)
        neg = neg_ids[rnd]
        counts = edge_counts[rnd]

        def one_bucket(item):
            return bucket_grads(item[0], item[1], theta, item[2], item[3], item[4], item[5], item[6])

        g_left, g_right, g_theta = lax.map(one_bucket, (lefts, rights, src, dst, rel, neg, counts))
        lefts = (lefts.astype(jnp.float32) - learn_rate * g_left).astype(jnp.bfloat16)
        rights = (rights.astype(jnp.float32) - learn_rate * g_right).astype(jnp.bfloat16)
        theta = theta - relation_rate * jnp.sum(g_theta, axis=0)
    return lefts.reshape(GROUPS * SLAB, W), rights.reshape(GROUPS * SLAB, W), theta
```

```python
import functools

import jax
import jax.numpy as jnp
from jax import lax
from jax.experimental import pallas as pl
from jax.experimental.pallas import tpu as pltpu
from jax.sharding import PartitionSpec as P

MESH = pl.DeviceIdType.MESH
F32, BF16, I32 = jnp.float32, jnp.bfloat16, jnp.int32
learn_rate = 0.05
relation_rate = 0.05


def nn(a, b):
    return lax.dot_general(a, b, (((1,), (0,)), ((), ())), preferred_element_type=F32)


def nt(a, b):
    return lax.dot_general(a, b, (((1,), (1,)), ((), ())), preferred_element_type=F32)


def hot(ids, rows):
    return lax.broadcasted_iota(I32, (rows, ids.shape[1]), 0) == ids


def as_bf16(mask):
    return jnp.where(mask, 1.0, 0.0).astype(BF16)


def sigmoid(x):
    return 0.5 * jnp.tanh(0.5 * x) + 0.5


def kernel(
    cfg,
    count_ref, left_in, right_in, theta_in, src_in, dst_in, rel_in, neg_in,
    left_out, right_out, theta_out,
    src_ref, dst_ref, rel_ref, neg_ref, theta,
    lf, rf, new_l, new_r, counts, turned, left_t, right_t, step_t,
    hrel, hsrc, t_ref, s_ref, q_ref, w_ref, u_ref, gs_ref,
    own_l, own_r, gls, grs, glr, grr, moved,
    gts, gown, pair_in, pair_sum, rs_in, xr, ag,
    sem_in, sem_out, sem_l, sem_r, sem_gl, sem_gr, sem_pair, sem_rs, sem_x, sem_ag, sem_fw,
):
    rounds, nb, ne, blocks, span, per, pieces = cfg
    rows, width = left_in.shape
    slab = rows * ne
    rels = theta_in.shape[0]
    half = rels // 2
    members = 4 * ne
    twins = nb // 8
    share = half // pieces // members
    edges = span * per
    slots = span * blocks
    b, e = lax.axis_index("bucket"), lax.axis_index("edge")
    core, y = lax.rem(b, 2), lax.rem(b // 2, 2)
    low, high = lax.rem(b // 4, 2), b // 8
    me = (low * 2 + y) * ne + e
    mate = {"bucket": b + 1 - 2 * core, "edge": e}
    ahead, behind = lax.rem(b + 1, nb), lax.rem(b + nb - 1, nb)

    near = [(dz, dy, de) for dz in range(2) for dy in range(2) for de in range(ne)][1:]
    near.sort(key=lambda d: -(d[0] + d[1] + min(d[2], ne - d[2])))

    def member(d):
        dz, dy, de = d
        zz, yy, ee = lax.rem(low + dz, 2), lax.rem(y + dy, 2), lax.rem(e + de, ne)
        return (zz * 2 + yy) * ne + ee, {"bucket": ((high * 2 + zz) * 2 + yy) * 2 + core, "edge": ee}

    def slot_of(d):
        return (d[0] * 2 + d[1]) * ne + d[2]

    def twin(d):
        return {"bucket": ((lax.rem(high + d, twins) * 2 + low) * 2 + y) * 2 + core, "edge": e}

    def edge_at(d):
        return lax.rem(e + d, ne)

    started = []

    def remote(src, dst, sems, to):
        return pltpu.make_async_remote_copy(
            src_ref=src, dst_ref=dst, send_sem=sems.at[0], recv_sem=sems.at[1],
            device_id=to, device_id_type=MESH,
        )

    def send(src, dst, sems, to):
        copy = remote(src, dst, sems, to)
        copy.start()
        started.append(copy)
        return copy

    barrier = pltpu.get_barrier_semaphore()
    greeted = [mate] + [member(d)[1] for d in near] + [twin(d) for d in range(1, twins)]
    for d in range(ne):
        for other in (ahead, behind):
            greeted.append({"bucket": other, "edge": edge_at(d)})
    for to in greeted:
        pl.semaphore_signal(barrier, inc=1, device_id=to, device_id_type=MESH)

    loads = [
        pltpu.make_async_copy(src, dst, sem_in.at[i])
        for i, (src, dst) in enumerate((
            (neg_in, neg_ref), (left_in, lf.at[0, e]), (right_in, rf.at[0, e]), (theta_in, theta),
            (rel_in, rel_ref), (src_in, src_ref), (dst_in, dst_ref),
        ))
    ]
    for copy in loads:
        copy.start()

    eye = as_bf16(lax.broadcasted_iota(I32, (width, width), 0) == lax.broadcasted_iota(I32, (width, width), 1))

    def over_edges(step):
        def one(i, carry):
            step(i, pl.ds(pl.multiple_of(i * edges, edges), edges))
            return carry

        lax.fori_loop(0, blocks // per, one, 0)

    def count_round(r):
        ones = jnp.ones((neg_ref.shape[3], 128), BF16)

        def one(i, carry):
            for j in range(per):
                ids = neg_ref[r, 0, pl.ds(i * per + j, 1), :]
                counts[r, i * per + j] = nn(as_bf16(hot(ids, slab)), ones)
            return carry

        lax.fori_loop(0, blocks // per, one, 0)

    def turn():
        wide = theta[...]
        top = wide.astype(BF16)
        rest = (wide - top.astype(F32)).astype(BF16)
        turned[pl.ds(0, width), :] = nt(eye, top).astype(BF16)
        turned[pl.ds(width, width), :] = nt(eye, rest).astype(BF16)

    def gather_theta(r):
        def step(i, at):
            at_rel = as_bf16(hot(rel_ref[r, :, at], rels))
            hrel[:, at] = at_rel
            both = nn(turned[...], at_rel)
            t_ref[:, at] = both[:width] + both[width:]

        over_edges(step)

    def mark_sources(r):
        def step(i, at):
            hsrc[:, at] = as_bf16(hot(src_ref[r, :, at], slab))

        over_edges(step)

    def gather_left():
        def step(i, at):
            s_ref[:, at] = nn(left_t[...], hsrc[:, at])

        over_edges(step)

    def score(r):
        live_to = count_ref[0, r]

        def step(i, at):
            slot = (e * blocks + i * per) * span + lax.broadcasted_iota(I32, (1, edges), 1)
            live = jnp.where(slot < live_to, 1.0, 0.0)
            at_dst = hot(dst_ref[r, :, at], slab)
            s, t = s_ref[:, at], t_ref[:, at]
            if r > 0:
                t = t - relation_rate * nn(step_t[...], hrel[:, at])
            q = (s * t).astype(BF16)
            q_ref[:, at] = q
            scores = nn(rf[r].reshape(slab, width), q)
            pos = jnp.sum(jnp.where(at_dst, scores, 0.0), axis=0, keepdims=True)
            g_pos = -sigmoid(-pos) * live
            g_neg = (sigmoid(scores) * live).astype(BF16).astype(F32)
            many = jnp.concatenate(
                [counts[r, i * per + j] for j in range(per) for _ in range(span // 128)], axis=1
            )
            weight = (many * g_neg + jnp.where(at_dst, g_pos, 0.0)).astype(BF16)
            w_ref[:, at] = weight
            g_q = nn(right_t[...], weight)
            u_ref[:, at] = (g_q * s).astype(BF16)
            g_s = g_q * t
            top = g_s.astype(BF16)
            gs_ref[0, :, at] = top
            gs_ref[1, :, at] = (g_s - top.astype(F32)).astype(BF16)

        over_edges(step)

    def left_rows(j):
        at = pl.ds(pl.multiple_of(j * rows, rows), rows)
        return nt(hsrc[at, :], gs_ref[0]) + nt(hsrc[at, :], gs_ref[1])

    def right_rows(j):
        at = pl.ds(pl.multiple_of(j * rows, rows), rows)
        return nt(w_ref[at, :], q_ref[...])

    def rel_rows(h):
        at = pl.ds(pl.multiple_of(h * half, half), half)
        return nt(hrel[at, :], u_ref[...]).reshape(pieces, members, share, width)

    loads[0].wait()
    count_round(0)
    loads[1].wait()
    loads[2].wait()
    pl.semaphore_wait(barrier, len(greeted))
    arrive_l, arrive_r = [], []
    for d in range(1, ne):
        to = {"bucket": b, "edge": edge_at(d)}
        arrive_l.append(send(lf.at[0, e], lf.at[0, e], sem_l.at[0, d], to))
    for d in range(1, ne):
        to = {"bucket": b, "edge": edge_at(d)}
        arrive_r.append(send(rf.at[0, e], rf.at[0, e], sem_r.at[0, d], to))
    loads[3].wait()
    turn()
    loads[4].wait()
    gather_theta(0)
    loads[5].wait()
    mark_sources(0)
    loads[6].wait()

    outs = []

    for r in range(rounds):
        last = r == rounds - 1
        if r == 0:
            for copy in arrive_l:
                copy.wait_recv()
            left_t[...] = nt(eye, lf[r].reshape(slab, width)).astype(BF16)
            gather_left()
            for copy in arrive_r:
                copy.wait_recv()
            right_t[...] = nt(eye, rf[r].reshape(slab, width)).astype(BF16)
        arrive_l, arrive_r = [], []
        score(r)

        gts[r] = rel_rows(1 - core).astype(BF16)
        pairs = [send(gts.at[r, p], pair_in.at[r, p], sem_pair.at[r, p], mate) for p in range(pieces)]
        gown[...] = rel_rows(core)
        shares = [[] for _ in range(pieces)]
        for p in range(pieces):
            pairs[p].wait_recv()
            pair_sum[r, p] = (gown[p] + pair_in[r, p].astype(F32)).astype(BF16)
            for d in near:
                c, to = member(d)
                copy = remote(pair_sum.at[r, p, c], rs_in.at[r, p, slot_of(d)], sem_rs.at[r, p], to)
                copy.start()
                shares[p].append(copy)

        whole = ne == 2 and not last
        slabs_l, slabs_r = [], []
        if whole:
            to = {"bucket": b, "edge": edge_at(1)}
            own_r[...] = nt(w_ref[...], q_ref[...]).reshape(own_r.shape)
            grs[r] = own_r[...].astype(BF16)
            slabs_r.append(send(grs.at[r], grr.at[r], sem_gr.at[r, 1], to))
            own_l[...] = (nt(hsrc[...], gs_ref[0]) + nt(hsrc[...], gs_ref[1])).reshape(own_l.shape)
            gls[r] = own_l[...].astype(BF16)
            slabs_l.append(send(gls.at[r], glr.at[r], sem_gl.at[r, 1], to))
        else:
            for d in range(1, ne):
                to = {"bucket": b, "edge": edge_at(d)}
                grs[r, d] = right_rows(edge_at(d)).astype(BF16)
                slabs_r.append(send(grs.at[r, d], grr.at[r, d], sem_gr.at[r, d], to))
            for d in range(1, ne):
                to = {"bucket": b, "edge": edge_at(d)}
                gls[r, d] = left_rows(edge_at(d)).astype(BF16)
                slabs_l.append(send(gls.at[r, d], glr.at[r, d], sem_gl.at[r, d], to))
            own_l[0] = left_rows(e)
            own_r[0] = right_rows(e)
        if not last:
            count_round(r + 1)
            mark_sources(r + 1)

        def all_but_one(ref, sems):
            return remote(ref.at[pl.ds(1, members - 1)], ref.at[pl.ds(1, members - 1)], sems, mate)

        def arrived(copies, ref, sems):
            all_but_one(ref, sems).wait_recv()

        crossed = []
        for p in range(pieces):
            arrived(shares[p], rs_in.at[r, p], sem_rs.at[r, p])
            g = gown[p, me] + pair_in[r, p, me].astype(F32)
            for d in range(1, members):
                g = g + rs_in[r, p, d].astype(F32)
            xr[r, p, 0] = g
            crossed.append([
                send(xr.at[r, p, 0], xr.at[r, p, d], sem_x.at[r, p, d], twin(d)) for d in range(1, twins)
            ])

        if not last:
            if r > 0:
                turn()
            gather_theta(r + 1)

        spread = [[] for _ in range(pieces)]
        for p in range(pieces):
            for copy in crossed[p]:
                copy.wait_recv()
            g = jnp.zeros((share, width), F32)
            for a in range(twins):
                g = g + xr[r, p, lax.rem(high + twins - a, twins)]
            ag[r, core, p, me] = g.astype(BF16)
            for d in near:
                block = ag.at[r, core, p, me]
                copy = remote(block, block, sem_ag.at[r, p], member(d)[1])
                copy.start()
                spread[p].append(copy)

        def updated(held, own, others, copies, rate):
            for copy in copies:
                copy.wait_recv()
            g = own[...] if whole else own[0]
            if whole:
                g = g + others[r].astype(F32)
                return (held[r].astype(F32) - rate * g).astype(BF16)
            for d in range(1, ne):
                g = g + others[r, d].astype(F32)
            return (held[r, e].astype(F32) - rate * g).astype(BF16)

        fresh = updated(rf, own_r, grr, slabs_r, learn_rate)
        if last:
            new_r[...] = fresh
            outs.append(pltpu.make_async_copy(new_r, right_out, sem_out.at[1]))
            outs[-1].start()
        elif whole:
            moved[r] = fresh
            to = {"bucket": ahead, "edge": e}
            arrive_r.append(send(moved.at[r], rf.at[r + 1], sem_r.at[r + 1, 0], to))
        else:
            moved[r, 0] = fresh
            for d in range(ne):
                to = {"bucket": ahead, "edge": edge_at(d)}
                arrive_r.append(send(moved.at[r, 0], rf.at[r + 1, e], sem_r.at[r + 1, d], to))
        fresh = updated(lf, own_l, glr, slabs_l, learn_rate)
        if last:
            new_l[...] = fresh
            outs.append(pltpu.make_async_copy(new_l, left_out, sem_out.at[0]))
            outs[-1].start()
        elif whole:
            lf[r + 1] = fresh
        else:
            lf[r + 1, e] = fresh
            for d in range(1, ne):
                to = {"bucket": b, "edge": edge_at(d)}
                arrive_l.append(send(lf.at[r + 1, e], lf.at[r + 1, e], sem_l.at[r + 1, d], to))
        if not last:
            for copy in arrive_l:
                copy.wait_recv()
            left_t[...] = nt(eye, lf[r + 1].reshape(slab, width)).astype(BF16)
            gather_left()

        forwards = []
        for p in range(pieces):
            arrived(spread[p], ag.at[r, core, p], sem_ag.at[r, p])
            forwards.append(send(ag.at[r, core, p], ag.at[r, core, p], sem_fw.at[r, p], mate))
        for h in range(2):
            where = core if h == 0 else 1 - core
            if h == 1:
                for copy in forwards:
                    copy.wait_recv()
            at = pl.ds(pl.multiple_of(where * half, half), half)
            step = ag[r, where].reshape(half, width)
            theta[at, :] = theta[at, :] - relation_rate * step.astype(F32)
            if last:
                outs.append(pltpu.make_async_copy(theta.at[at], theta_out.at[at], sem_out.at[2 + h]))
                outs[-1].start()
        if not last:
            for copy in arrive_r:
                copy.wait_recv()
            right_t[...] = nt(eye, rf[r + 1].reshape(slab, width)).astype(BF16)
            step_t[...] = nt(eye, ag[r].reshape(rels, width)).astype(BF16)

    for copy in started:
        copy.wait_send()
    for r in range(rounds):
        for p in range(pieces):
            all_but_one(rs_in.at[r, p], sem_rs.at[r, p]).wait_send()
            all_but_one(ag.at[r, core, p], sem_ag.at[r, p]).wait_send()
    for copy in outs:
        copy.wait()


def finish(left_in, right_in, theta_in, left_out, right_out, theta_out, left, right, theta, sems):
    moves = ((left_in, left, left_out), (right_in, right, right_out), (theta_in, theta, theta_out))
    ins = [pltpu.make_async_copy(a, v, sems.at[0, i]) for i, (a, v, _) in enumerate(moves)]
    outs = [pltpu.make_async_copy(v, o, sems.at[1, i]) for i, (_, v, o) in enumerate(moves)]
    for copy in ins:
        copy.start()
    for a, o in zip(ins, outs):
        a.wait()
        o.start()
    for copy in outs:
        copy.wait()


def solution(mesh):
    nb, ne = mesh.shape["bucket"], mesh.shape["edge"]

    def body(left_slab, right_slab, relation, src_ids, dst_ids, rel_ids, neg_ids, edge_counts):
        rounds, _, blocks, negs = neg_ids.shape
        slots = src_ids.shape[2]
        span = slots // blocks
        rows, width = left_slab.shape
        slab, rels = rows * ne, relation.shape[0]
        half = rels // 2
        per = 4 if slab <= 512 else 1
        members, twins = 4 * ne, nb // 8
        pieces = max(1, min(2, half // (16 * members)))
        share = half // pieces // members
        held = ne if ne == 2 else 1
        vmem = pltpu.VMEM
        hbm = pl.BlockSpec(memory_space=pltpu.HBM)
        dma = pltpu.SemaphoreType.DMA
        cfg = (rounds, nb, ne, blocks, span, per, pieces)
        shares = (pieces, members, share, width)
        results = (
            jax.ShapeDtypeStruct((rows, width), BF16),
            jax.ShapeDtypeStruct((rows, width), BF16),
            jax.ShapeDtypeStruct((rels, width), F32),
        )
        left, right, theta = pl.pallas_call(
            functools.partial(kernel, cfg),
            out_shape=results,
            in_specs=[pl.BlockSpec(memory_space=pltpu.SMEM)] + [hbm] * 7,
            out_specs=(hbm, hbm, hbm),
            scratch_shapes=[
                vmem((rounds, 1, slots), I32),
                vmem((rounds, 1, slots), I32),
                vmem((rounds, 1, slots), I32),
                vmem((rounds, 1, blocks, negs), I32),
                vmem((rels, width), F32),
                vmem((rounds, ne, rows, width), BF16),
                vmem((rounds, ne, rows, width), BF16),
                vmem((rows, width), BF16),
                vmem((rows, width), BF16),
                vmem((rounds, blocks, slab, 128), F32),
                vmem((2 * width, rels), BF16),
                vmem((width, slab), BF16),
                vmem((width, slab), BF16),
                vmem((width, rels), BF16),
                vmem((rels, slots), BF16),
                vmem((slab, slots), BF16),
                vmem((width, slots), F32),
                vmem((width, slots), F32),
                vmem((width, slots), BF16),
                vmem((slab, slots), BF16),
                vmem((width, slots), BF16),
                vmem((2, width, slots), BF16),
                vmem((held, rows, width), F32),
                vmem((held, rows, width), F32),
                vmem((rounds, ne, rows, width), BF16),
                vmem((rounds, ne, rows, width), BF16),
                vmem((rounds, ne, rows, width), BF16),
                vmem((rounds, ne, rows, width), BF16),
                vmem((rounds, held, rows, width), BF16),
                vmem((rounds,) + shares, BF16),
                vmem(shares, F32),
                vmem((rounds,) + shares, BF16),
                vmem((rounds,) + shares, BF16),
                vmem((rounds,) + shares, BF16),
                vmem((rounds, pieces, twins, share, width), F32),
                vmem((rounds, 2) + shares, BF16),
                dma((7,)),
                dma((4,)),
                dma((rounds, ne, 2)),
                dma((rounds, ne, 2)),
                dma((rounds, ne, 2)),
                dma((rounds, ne, 2)),
                dma((rounds, pieces, 2)),
                dma((rounds, pieces, 2)),
                dma((rounds, pieces, twins, 2)),
                dma((rounds, pieces, 2)),
                dma((rounds, pieces, 2)),
            ],
            compiler_params=pltpu.CompilerParams(
                collective_id=0, has_side_effects=True, vmem_limit_bytes=60 * 1024 * 1024
            ),
        )(edge_counts.T, left_slab, right_slab, relation, src_ids, dst_ids, rel_ids, neg_ids)
        return pl.pallas_call(
            finish,
            out_shape=results,
            in_specs=[hbm] * 3,
            out_specs=(hbm, hbm, hbm),
            scratch_shapes=[
                vmem((rows, width), BF16),
                vmem((rows, width), BF16),
                vmem((rels, width), F32),
                dma((2, 3)),
            ],
            compiler_params=pltpu.CompilerParams(vmem_limit_bytes=63 * 1024 * 1024),
        )(left, right, theta)

    placed = (
        P(("bucket", "edge"), None),
        P(("bucket", "edge"), None),
        P(),
        P(None, "bucket", "edge"),
        P(None, "bucket", "edge"),
        P(None, "bucket", "edge"),
        P(None, "bucket", "edge", None),
        P(None, "bucket"),
    )
    return jax.shard_map(
        body,
        mesh=mesh,
        in_specs=placed,
        out_specs=(P(("bucket", "edge"), None), P(("bucket", "edge"), None), P()),
        check_vma=False,
    )
```

```python
import functools

import jax
import jax.numpy as jnp
from jax import lax
from jax.experimental import pallas as pl
from jax.experimental.pallas import tpu as pltpu
from jax.sharding import PartitionSpec as P

MESH = pl.DeviceIdType.MESH
F32, BF16, I32 = jnp.float32, jnp.bfloat16, jnp.int32
learn_rate = 0.05
relation_rate = 0.05


def nn(a, b):
    return lax.dot_general(a, b, (((1,), (0,)), ((), ())), preferred_element_type=F32)


def nt(a, b):
    return lax.dot_general(a, b, (((1,), (1,)), ((), ())), preferred_element_type=F32)


def hot(ids, rows):
    return lax.broadcasted_iota(I32, (rows, ids.shape[1]), 0) == ids


def as_bf16(mask):
    return jnp.where(mask, 1.0, 0.0).astype(BF16)


def sigmoid(x):
    return 0.5 * jnp.tanh(0.5 * x) + 0.5


def kernel(
    cfg,
    count_ref, left_in, right_in, theta_in, src_in, dst_in, rel_in, neg_in,
    left_out, right_out, theta_out,
    src_ref, dst_ref, rel_ref, neg_ref, theta,
    lf, rf, new_l, new_r, counts, turned, left_t, right_t, step_t,
    hrel, hsrc, t_ref, s_ref, q_ref, w_ref, u_ref, gs_ref,
    own_l, own_r, gls, grs, glr, grr, moved,
    gts, gown, pair_in, pair_sum, rs_in, xr, ag,
    sem_in, sem_out, sem_l, sem_r, sem_gl, sem_gr, sem_pair, sem_rs, sem_x, sem_ag, sem_fw,
):
    rounds, nb, ne, blocks, span, per, pieces = cfg
    rows, width = left_in.shape
    slab = rows * ne
    rels = theta_in.shape[0]
    half = rels // 2
    members = 4 * ne
    twins = nb // 8
    share = half // pieces // members
    edges = span * per
    slots = span * blocks
    b, e = lax.axis_index("bucket"), lax.axis_index("edge")
    core, y = lax.rem(b, 2), lax.rem(b // 2, 2)
    low, high = lax.rem(b // 4, 2), b // 8
    me = (low * 2 + y) * ne + e
    mate = {"bucket": b + 1 - 2 * core, "edge": e}
    ahead, behind = lax.rem(b + 1, nb), lax.rem(b + nb - 1, nb)

    near = [(dz, dy, de) for dz in range(2) for dy in range(2) for de in range(ne)][1:]
    near.sort(key=lambda d: -(d[0] + d[1] + min(d[2], ne - d[2])))

    def member(d):
        dz, dy, de = d
        zz, yy, ee = lax.rem(low + dz, 2), lax.rem(y + dy, 2), lax.rem(e + de, ne)
        return (zz * 2 + yy) * ne + ee, {"bucket": ((high * 2 + zz) * 2 + yy) * 2 + core, "edge": ee}

    def slot_of(d):
        return (d[0] * 2 + d[1]) * ne + d[2]

    def twin(d):
        return {"bucket": ((lax.rem(high + d, twins) * 2 + low) * 2 + y) * 2 + core, "edge": e}

    def edge_at(d):
        return lax.rem(e + d, ne)

    started = []

    def remote(src, dst, sems, to):
        return pltpu.make_async_remote_copy(
            src_ref=src, dst_ref=dst, send_sem=sems.at[0], recv_sem=sems.at[1],
            device_id=to, device_id_type=MESH,
        )

    def send(src, dst, sems, to):
        copy = remote(src, dst, sems, to)
        copy.start()
        started.append(copy)
        return copy

    barrier = pltpu.get_barrier_semaphore()
    greeted = [mate] + [member(d)[1] for d in near] + [twin(d) for d in range(1, twins)]
    for d in range(ne):
        for other in (ahead, behind):
            greeted.append({"bucket": other, "edge": edge_at(d)})
    for to in greeted:
        pl.semaphore_signal(barrier, inc=1, device_id=to, device_id_type=MESH)

    loads = [
        pltpu.make_async_copy(src, dst, sem_in.at[i])
        for i, (src, dst) in enumerate((
            (neg_in, neg_ref), (left_in, lf.at[0, e]), (right_in, rf.at[0, e]), (theta_in, theta),
            (rel_in, rel_ref), (src_in, src_ref), (dst_in, dst_ref),
        ))
    ]
    for copy in loads:
        copy.start()

    eye = as_bf16(lax.broadcasted_iota(I32, (width, width), 0) == lax.broadcasted_iota(I32, (width, width), 1))

    def over_edges(step):
        def one(i, carry):
            step(i, pl.ds(pl.multiple_of(i * edges, edges), edges))
            return carry

        lax.fori_loop(0, blocks // per, one, 0)

    def count_round(r):
        ones = jnp.ones((neg_ref.shape[3], 128), BF16)

        def one(i, carry):
            for j in range(per):
                ids = neg_ref[r, 0, pl.ds(i * per + j, 1), :]
                counts[r, i * per + j] = nn(as_bf16(hot(ids, slab)), ones)
            return carry

        lax.fori_loop(0, blocks // per, one, 0)

    def turn():
        wide = theta[...]
        top = wide.astype(BF16)
        rest = (wide - top.astype(F32)).astype(BF16)
        turned[pl.ds(0, width), :] = nt(eye, top).astype(BF16)
        turned[pl.ds(width, width), :] = nt(eye, rest).astype(BF16)

    def gather_theta(r):
        def step(i, at):
            at_rel = as_bf16(hot(rel_ref[r, :, at], rels))
            hrel[:, at] = at_rel
            both = nn(turned[...], at_rel)
            t_ref[:, at] = both[:width] + both[width:]

        over_edges(step)

    def mark_sources(r):
        def step(i, at):
            hsrc[:, at] = as_bf16(hot(src_ref[r, :, at], slab))

        over_edges(step)

    def gather_left():
        def step(i, at):
            s_ref[:, at] = nn(left_t[...], hsrc[:, at])

        over_edges(step)

    def weigh(r, then=None):
        live_to = count_ref[0, r]

        def step(i, at):
            slot = (e * blocks + i * per) * span + lax.broadcasted_iota(I32, (1, edges), 1)
            live = jnp.where(slot < live_to, 1.0, 0.0)
            at_dst = hot(dst_ref[r, :, at], slab)
            s, t = s_ref[:, at], t_ref[:, at]
            if r > 0:
                t = t - relation_rate * nn(step_t[...], hrel[:, at])
                t_ref[:, at] = t
            q = (s * t).astype(BF16)
            q_ref[:, at] = q
            scores = nn(rf[r].reshape(slab, width), q)
            pos = jnp.sum(jnp.where(at_dst, scores, 0.0), axis=0, keepdims=True)
            g_pos = -sigmoid(-pos) * live
            g_neg = (sigmoid(scores) * live).astype(BF16).astype(F32)
            many = jnp.concatenate(
                [counts[r, i * per + j] for j in range(per) for _ in range(span // 128)], axis=1
            )
            weight = (many * g_neg + jnp.where(at_dst, g_pos, 0.0)).astype(BF16)
            w_ref[:, at] = weight
            if then:
                then(at, s, t, weight)

        over_edges(step)

    def back(at, s, t, weight):
        g_q = nn(right_t[...], weight)
        u_ref[:, at] = (g_q * s).astype(BF16)
        g_s = g_q * t
        top = g_s.astype(BF16)
        gs_ref[0, :, at] = top
        gs_ref[1, :, at] = (g_s - top.astype(F32)).astype(BF16)

    def left_rows(j):
        at = pl.ds(pl.multiple_of(j * rows, rows), rows)
        return nt(hsrc[at, :], gs_ref[0]) + nt(hsrc[at, :], gs_ref[1])

    def right_rows(j):
        at = pl.ds(pl.multiple_of(j * rows, rows), rows)
        return nt(w_ref[at, :], q_ref[...])

    def rel_rows(h):
        at = pl.ds(pl.multiple_of(h * half, half), half)
        return nt(hrel[at, :], u_ref[...]).reshape(pieces, members, share, width)

    loads[0].wait()
    count_round(0)
    loads[1].wait()
    loads[2].wait()
    pl.semaphore_wait(barrier, len(greeted))
    arrive_l, arrive_r = [], []
    for d in range(1, ne):
        to = {"bucket": b, "edge": edge_at(d)}
        arrive_l.append(send(lf.at[0, e], lf.at[0, e], sem_l.at[0, d], to))
    for d in range(1, ne):
        to = {"bucket": b, "edge": edge_at(d)}
        arrive_r.append(send(rf.at[0, e], rf.at[0, e], sem_r.at[0, d], to))
    loads[3].wait()
    turn()
    loads[4].wait()
    gather_theta(0)
    loads[5].wait()
    mark_sources(0)
    loads[6].wait()

    outs = []

    for r in range(rounds):
        last = r == rounds - 1
        if r == 0:
            for copy in arrive_l:
                copy.wait_recv()
            left_t[...] = nt(eye, lf[r].reshape(slab, width)).astype(BF16)
            gather_left()
            for copy in arrive_r:
                copy.wait_recv()
            right_t[...] = nt(eye, rf[r].reshape(slab, width)).astype(BF16)
        arrive_l, arrive_r = [], []
        whole = ne == 2 and not last
        slabs_l, slabs_r = [], []
        if whole:
            weigh(r)
            to = {"bucket": b, "edge": edge_at(1)}
            own_r[...] = nt(w_ref[...], q_ref[...]).reshape(own_r.shape)
            grs[r] = own_r[...].astype(BF16)
            slabs_r.append(send(grs.at[r], grr.at[r], sem_gr.at[r, 1], to))
            over_edges(lambda i, at: back(at, s_ref[:, at], t_ref[:, at], w_ref[:, at]))
        else:
            weigh(r, back)

        gts[r] = rel_rows(1 - core).astype(BF16)
        pairs = [send(gts.at[r, p], pair_in.at[r, p], sem_pair.at[r, p], mate) for p in range(pieces)]
        gown[...] = rel_rows(core)
        shares = [[] for _ in range(pieces)]
        for p in range(pieces):
            pairs[p].wait_recv()
            pair_sum[r, p] = (gown[p] + pair_in[r, p].astype(F32)).astype(BF16)
            for d in near:
                c, to = member(d)
                copy = remote(pair_sum.at[r, p, c], rs_in.at[r, p, slot_of(d)], sem_rs.at[r, p], to)
                copy.start()
                shares[p].append(copy)

        if whole:
            to = {"bucket": b, "edge": edge_at(1)}
            own_l[...] = (nt(hsrc[...], gs_ref[0]) + nt(hsrc[...], gs_ref[1])).reshape(own_l.shape)
            gls[r] = own_l[...].astype(BF16)
            slabs_l.append(send(gls.at[r], glr.at[r], sem_gl.at[r, 1], to))
        else:
            for d in range(1, ne):
                to = {"bucket": b, "edge": edge_at(d)}
                grs[r, d] = right_rows(edge_at(d)).astype(BF16)
                slabs_r.append(send(grs.at[r, d], grr.at[r, d], sem_gr.at[r, d], to))
            for d in range(1, ne):
                to = {"bucket": b, "edge": edge_at(d)}
                gls[r, d] = left_rows(edge_at(d)).astype(BF16)
                slabs_l.append(send(gls.at[r, d], glr.at[r, d], sem_gl.at[r, d], to))
            own_l[0] = left_rows(e)
            own_r[0] = right_rows(e)
        if not last:
            count_round(r + 1)
            mark_sources(r + 1)

        def all_but_one(ref, sems):
            return remote(ref.at[pl.ds(1, members - 1)], ref.at[pl.ds(1, members - 1)], sems, mate)

        def arrived(copies, ref, sems):
            all_but_one(ref, sems).wait_recv()

        crossed = []
        for p in range(pieces):
            arrived(shares[p], rs_in.at[r, p], sem_rs.at[r, p])
            g = gown[p, me] + pair_in[r, p, me].astype(F32)
            for d in range(1, members):
                g = g + rs_in[r, p, d].astype(F32)
            xr[r, p, 0] = g
            crossed.append([
                send(xr.at[r, p, 0], xr.at[r, p, d], sem_x.at[r, p, d], twin(d)) for d in range(1, twins)
            ])

        if not last:
            if r > 0:
                turn()
            gather_theta(r + 1)

        spread = [[] for _ in range(pieces)]
        for p in range(pieces):
            for copy in crossed[p]:
                copy.wait_recv()
            g = jnp.zeros((share, width), F32)
            for a in range(twins):
                g = g + xr[r, p, lax.rem(high + twins - a, twins)]
            ag[r, core, p, me] = g.astype(BF16)
            for d in near:
                block = ag.at[r, core, p, me]
                copy = remote(block, block, sem_ag.at[r, p], member(d)[1])
                copy.start()
                spread[p].append(copy)

        def updated(held, own, others, copies, rate):
            for copy in copies:
                copy.wait_recv()
            g = own[...] if whole else own[0]
            if whole:
                g = g + others[r].astype(F32)
                return (held[r].astype(F32) - rate * g).astype(BF16)
            for d in range(1, ne):
                g = g + others[r, d].astype(F32)
            return (held[r, e].astype(F32) - rate * g).astype(BF16)

        fresh = updated(rf, own_r, grr, slabs_r, learn_rate)
        if last:
            new_r[...] = fresh
            outs.append(pltpu.make_async_copy(new_r, right_out, sem_out.at[1]))
            outs[-1].start()
        elif whole:
            moved[r] = fresh
            to = {"bucket": ahead, "edge": e}
            arrive_r.append(send(moved.at[r], rf.at[r + 1], sem_r.at[r + 1, 0], to))
        else:
            moved[r, 0] = fresh
            for d in range(ne):
                to = {"bucket": ahead, "edge": edge_at(d)}
                arrive_r.append(send(moved.at[r, 0], rf.at[r + 1, e], sem_r.at[r + 1, d], to))
        fresh = updated(lf, own_l, glr, slabs_l, learn_rate)
        if last:
            new_l[...] = fresh
            outs.append(pltpu.make_async_copy(new_l, left_out, sem_out.at[0]))
            outs[-1].start()
        elif whole:
            lf[r + 1] = fresh
        else:
            lf[r + 1, e] = fresh
            for d in range(1, ne):
                to = {"bucket": b, "edge": edge_at(d)}
                arrive_l.append(send(lf.at[r + 1, e], lf.at[r + 1, e], sem_l.at[r + 1, d], to))
        if not last:
            for copy in arrive_l:
                copy.wait_recv()
            left_t[...] = nt(eye, lf[r + 1].reshape(slab, width)).astype(BF16)
            gather_left()

        forwards = []
        for p in range(pieces):
            arrived(spread[p], ag.at[r, core, p], sem_ag.at[r, p])
            forwards.append(send(ag.at[r, core, p], ag.at[r, core, p], sem_fw.at[r, p], mate))
        for h in range(2):
            where = core if h == 0 else 1 - core
            if h == 1:
                for copy in forwards:
                    copy.wait_recv()
            at = pl.ds(pl.multiple_of(where * half, half), half)
            step = ag[r, where].reshape(half, width)
            theta[at, :] = theta[at, :] - relation_rate * step.astype(F32)
            if last:
                outs.append(pltpu.make_async_copy(theta.at[at], theta_out.at[at], sem_out.at[2 + h]))
                outs[-1].start()
        if not last:
            for copy in arrive_r:
                copy.wait_recv()
            right_t[...] = nt(eye, rf[r + 1].reshape(slab, width)).astype(BF16)
            step_t[...] = nt(eye, ag[r].reshape(rels, width)).astype(BF16)

    for copy in started:
        copy.wait_send()
    for r in range(rounds):
        for p in range(pieces):
            all_but_one(rs_in.at[r, p], sem_rs.at[r, p]).wait_send()
            all_but_one(ag.at[r, core, p], sem_ag.at[r, p]).wait_send()
    for copy in outs:
        copy.wait()


def finish(left_in, right_in, theta_in, left_out, right_out, theta_out, left, right, theta, sems):
    moves = ((left_in, left, left_out), (right_in, right, right_out), (theta_in, theta, theta_out))
    ins = [pltpu.make_async_copy(a, v, sems.at[0, i]) for i, (a, v, _) in enumerate(moves)]
    outs = [pltpu.make_async_copy(v, o, sems.at[1, i]) for i, (_, v, o) in enumerate(moves)]
    for copy in ins:
        copy.start()
    for a, o in zip(ins, outs):
        a.wait()
        o.start()
    for copy in outs:
        copy.wait()


def solution(mesh):
    nb, ne = mesh.shape["bucket"], mesh.shape["edge"]

    def body(left_slab, right_slab, relation, src_ids, dst_ids, rel_ids, neg_ids, edge_counts):
        rounds, _, blocks, negs = neg_ids.shape
        slots = src_ids.shape[2]
        span = slots // blocks
        rows, width = left_slab.shape
        slab, rels = rows * ne, relation.shape[0]
        half = rels // 2
        per = 4 if slab <= 512 else 1
        members, twins = 4 * ne, nb // 8
        pieces = max(1, min(2, half // (16 * members)))
        share = half // pieces // members
        held = ne if ne == 2 else 1
        vmem = pltpu.VMEM
        hbm = pl.BlockSpec(memory_space=pltpu.HBM)
        dma = pltpu.SemaphoreType.DMA
        cfg = (rounds, nb, ne, blocks, span, per, pieces)
        shares = (pieces, members, share, width)
        results = (
            jax.ShapeDtypeStruct((rows, width), BF16),
            jax.ShapeDtypeStruct((rows, width), BF16),
            jax.ShapeDtypeStruct((rels, width), F32),
        )
        left, right, theta = pl.pallas_call(
            functools.partial(kernel, cfg),
            out_shape=results,
            in_specs=[pl.BlockSpec(memory_space=pltpu.SMEM)] + [hbm] * 7,
            out_specs=(hbm, hbm, hbm),
            scratch_shapes=[
                vmem((rounds, 1, slots), I32),
                vmem((rounds, 1, slots), I32),
                vmem((rounds, 1, slots), I32),
                vmem((rounds, 1, blocks, negs), I32),
                vmem((rels, width), F32),
                vmem((rounds, ne, rows, width), BF16),
                vmem((rounds, ne, rows, width), BF16),
                vmem((rows, width), BF16),
                vmem((rows, width), BF16),
                vmem((rounds, blocks, slab, 128), F32),
                vmem((2 * width, rels), BF16),
                vmem((width, slab), BF16),
                vmem((width, slab), BF16),
                vmem((width, rels), BF16),
                vmem((rels, slots), BF16),
                vmem((slab, slots), BF16),
                vmem((width, slots), F32),
                vmem((width, slots), F32),
                vmem((width, slots), BF16),
                vmem((slab, slots), BF16),
                vmem((width, slots), BF16),
                vmem((2, width, slots), BF16),
                vmem((held, rows, width), F32),
                vmem((held, rows, width), F32),
                vmem((rounds, ne, rows, width), BF16),
                vmem((rounds, ne, rows, width), BF16),
                vmem((rounds, ne, rows, width), BF16),
                vmem((rounds, ne, rows, width), BF16),
                vmem((rounds, held, rows, width), BF16),
                vmem((rounds,) + shares, BF16),
                vmem(shares, F32),
                vmem((rounds,) + shares, BF16),
                vmem((rounds,) + shares, BF16),
                vmem((rounds,) + shares, BF16),
                vmem((rounds, pieces, twins, share, width), F32),
                vmem((rounds, 2) + shares, BF16),
                dma((7,)),
                dma((4,)),
                dma((rounds, ne, 2)),
                dma((rounds, ne, 2)),
                dma((rounds, ne, 2)),
                dma((rounds, ne, 2)),
                dma((rounds, pieces, 2)),
                dma((rounds, pieces, 2)),
                dma((rounds, pieces, twins, 2)),
                dma((rounds, pieces, 2)),
                dma((rounds, pieces, 2)),
            ],
            compiler_params=pltpu.CompilerParams(
                collective_id=0, has_side_effects=True, vmem_limit_bytes=60 * 1024 * 1024
            ),
        )(edge_counts.T, left_slab, right_slab, relation, src_ids, dst_ids, rel_ids, neg_ids)
        return pl.pallas_call(
            finish,
            out_shape=results,
            in_specs=[hbm] * 3,
            out_specs=(hbm, hbm, hbm),
            scratch_shapes=[
                vmem((rows, width), BF16),
                vmem((rows, width), BF16),
                vmem((rels, width), F32),
                dma((2, 3)),
            ],
            compiler_params=pltpu.CompilerParams(vmem_limit_bytes=63 * 1024 * 1024),
        )(left, right, theta)

    placed = (
        P(("bucket", "edge"), None),
        P(("bucket", "edge"), None),
        P(),
        P(None, "bucket", "edge"),
        P(None, "bucket", "edge"),
        P(None, "bucket", "edge"),
        P(None, "bucket", "edge", None),
        P(None, "bucket"),
    )
    return jax.shard_map(
        body,
        mesh=mesh,
        in_specs=placed,
        out_specs=(P(("bucket", "edge"), None), P(("bucket", "edge"), None), P()),
        check_vma=False,
    )
```

```python
import functools

import jax
import jax.numpy as jnp
from jax import lax
from jax.experimental import pallas as pl
from jax.experimental.pallas import tpu as pltpu
from jax.sharding import PartitionSpec as P

MESH = pl.DeviceIdType.MESH
F32, BF16, I32 = jnp.float32, jnp.bfloat16, jnp.int32
learn_rate = 0.05
relation_rate = 0.05


def nn(a, b):
    return lax.dot_general(a, b, (((1,), (0,)), ((), ())), preferred_element_type=F32)


def nt(a, b):
    return lax.dot_general(a, b, (((1,), (1,)), ((), ())), preferred_element_type=F32)


def hot(ids, rows):
    return lax.broadcasted_iota(I32, (rows, ids.shape[1]), 0) == ids


def as_bf16(mask):
    return jnp.where(mask, 1.0, 0.0).astype(BF16)


def sigmoid(x):
    return 0.5 * jnp.tanh(0.5 * x) + 0.5


def kernel(
    cfg,
    count_ref, left_in, right_in, theta_in, src_in, dst_in, rel_in, neg_in,
    left_out, right_out, theta_out,
    src_ref, dst_ref, rel_ref, neg_ref, theta,
    lf, rf, new_l, new_r, counts, turned, left_t, right_t, step_t,
    hrel, hsrc, t_ref, s_ref, q_ref, w_ref, u_ref, gs_ref,
    own_l, own_r, gls, grs, glr, grr, moved,
    gts, gown, pair_in, pair_sum, rs_in, xr, ag,
    sem_in, sem_out, sem_l, sem_r, sem_gl, sem_gr, sem_pair, sem_rs, sem_x, sem_ag, sem_fw,
):
    rounds, nb, ne, blocks, span, per, pieces = cfg
    rows, width = left_in.shape
    slab = rows * ne
    rels = theta_in.shape[0]
    half = rels // 2
    members = 4 * ne
    twins = nb // 8
    share = half // pieces // members
    edges = span * per
    slots = span * blocks
    b, e = lax.axis_index("bucket"), lax.axis_index("edge")
    core, y = lax.rem(b, 2), lax.rem(b // 2, 2)
    low, high = lax.rem(b // 4, 2), b // 8
    me = (low * 2 + y) * ne + e
    mate = {"bucket": b + 1 - 2 * core, "edge": e}
    ahead, behind = lax.rem(b + 1, nb), lax.rem(b + nb - 1, nb)

    near = [(dz, dy, de) for dz in range(2) for dy in range(2) for de in range(ne)][1:]
    near.sort(key=lambda d: -(d[0] + d[1] + min(d[2], ne - d[2])))

    def member(d):
        dz, dy, de = d
        zz, yy, ee = lax.rem(low + dz, 2), lax.rem(y + dy, 2), lax.rem(e + de, ne)
        return (zz * 2 + yy) * ne + ee, {"bucket": ((high * 2 + zz) * 2 + yy) * 2 + core, "edge": ee}

    def slot_of(d):
        return (d[0] * 2 + d[1]) * ne + d[2]

    def twin(d):
        return {"bucket": ((lax.rem(high + d, twins) * 2 + low) * 2 + y) * 2 + core, "edge": e}

    def edge_at(d):
        return lax.rem(e + d, ne)

    started = []

    def remote(src, dst, sems, to):
        return pltpu.make_async_remote_copy(
            src_ref=src, dst_ref=dst, send_sem=sems.at[0], recv_sem=sems.at[1],
            device_id=to, device_id_type=MESH,
        )

    def send(src, dst, sems, to):
        copy = remote(src, dst, sems, to)
        copy.start()
        started.append(copy)
        return copy

    barrier = pltpu.get_barrier_semaphore()
    greeted = [mate] + [member(d)[1] for d in near] + [twin(d) for d in range(1, twins)]
    for d in range(ne):
        for other in (ahead, behind):
            greeted.append({"bucket": other, "edge": edge_at(d)})
    for to in greeted:
        pl.semaphore_signal(barrier, inc=1, device_id=to, device_id_type=MESH)

    loads = [
        pltpu.make_async_copy(src, dst, sem_in.at[i])
        for i, (src, dst) in enumerate((
            (neg_in, neg_ref), (left_in, lf.at[0, e]), (right_in, rf.at[0, e]), (theta_in, theta),
            (rel_in, rel_ref), (src_in, src_ref), (dst_in, dst_ref),
        ))
    ]
    for copy in loads:
        copy.start()

    eye = as_bf16(lax.broadcasted_iota(I32, (width, width), 0) == lax.broadcasted_iota(I32, (width, width), 1))

    def over_edges(step):
        def one(i, carry):
            step(i, pl.ds(pl.multiple_of(i * edges, edges), edges))
            return carry

        lax.fori_loop(0, blocks // per, one, 0)

    def count_round(r):
        ones = jnp.ones((neg_ref.shape[3], 128), BF16)

        def one(i, carry):
            for j in range(per):
                ids = neg_ref[r, 0, pl.ds(i * per + j, 1), :]
                counts[r, i * per + j] = nn(as_bf16(hot(ids, slab)), ones)
            return carry

        lax.fori_loop(0, blocks // per, one, 0)

    def turn():
        wide = theta[...]
        top = wide.astype(BF16)
        rest = (wide - top.astype(F32)).astype(BF16)
        turned[pl.ds(0, width), :] = nt(eye, top).astype(BF16)
        turned[pl.ds(width, width), :] = nt(eye, rest).astype(BF16)

    def gather_theta(r):
        def step(i, at):
            at_rel = as_bf16(hot(rel_ref[r, :, at], rels))
            hrel[:, at] = at_rel
            both = nn(turned[...], at_rel)
            t_ref[:, at] = both[:width] + both[width:]

        over_edges(step)

    def mark_sources(r):
        def step(i, at):
            hsrc[:, at] = as_bf16(hot(src_ref[r, :, at], slab))

        over_edges(step)

    def gather_left():
        def step(i, at):
            s_ref[:, at] = nn(left_t[...], hsrc[:, at])

        over_edges(step)

    def moved_by(h, at):
        of = pl.ds(pl.multiple_of(h * half, half), half)
        return relation_rate * nn(step_t[h], hrel[of, at])

    def take_step(i, at):
        t_ref[:, at] = t_ref[:, at] - moved_by(core, at)

    def weigh(r, then=None):
        live_to = count_ref[0, r]

        def step(i, at):
            slot = (e * blocks + i * per) * span + lax.broadcasted_iota(I32, (1, edges), 1)
            live = jnp.where(slot < live_to, 1.0, 0.0)
            at_dst = hot(dst_ref[r, :, at], slab)
            s, t = s_ref[:, at], t_ref[:, at]
            if r > 0:
                t = t - moved_by(1 - core, at)
                t_ref[:, at] = t
            q = (s * t).astype(BF16)
            q_ref[:, at] = q
            scores = nn(rf[r].reshape(slab, width), q)
            pos = jnp.sum(jnp.where(at_dst, scores, 0.0), axis=0, keepdims=True)
            g_pos = -sigmoid(-pos) * live
            g_neg = (sigmoid(scores) * live).astype(BF16).astype(F32)
            many = jnp.concatenate(
                [counts[r, i * per + j] for j in range(per) for _ in range(span // 128)], axis=1
            )
            weight = (many * g_neg + jnp.where(at_dst, g_pos, 0.0)).astype(BF16)
            w_ref[:, at] = weight
            if then:
                then(at, s, t, weight)

        over_edges(step)

    def back(at, s, t, weight):
        g_q = nn(right_t[...], weight)
        u_ref[:, at] = (g_q * s).astype(BF16)
        g_s = g_q * t
        top = g_s.astype(BF16)
        gs_ref[0, :, at] = top

    def left_rows(j):
        at = pl.ds(pl.multiple_of(j * rows, rows), rows)
        return nt(hsrc[at, :], gs_ref[0])

    def right_rows(j):
        at = pl.ds(pl.multiple_of(j * rows, rows), rows)
        return nt(w_ref[at, :], q_ref[...])

    def rel_rows(h):
        at = pl.ds(pl.multiple_of(h * half, half), half)
        return nt(hrel[at, :], u_ref[...]).reshape(pieces, members, share, width)

    loads[0].wait()
    count_round(0)
    loads[1].wait()
    loads[2].wait()
    pl.semaphore_wait(barrier, len(greeted))
    arrive_l, arrive_r = [], []
    for d in range(1, ne):
        to = {"bucket": b, "edge": edge_at(d)}
        arrive_l.append(send(lf.at[0, e], lf.at[0, e], sem_l.at[0, d], to))
    for d in range(1, ne):
        to = {"bucket": b, "edge": edge_at(d)}
        arrive_r.append(send(rf.at[0, e], rf.at[0, e], sem_r.at[0, d], to))
    loads[3].wait()
    turn()
    loads[4].wait()
    gather_theta(0)
    loads[5].wait()
    mark_sources(0)
    loads[6].wait()

    outs = []

    for r in range(rounds):
        last = r == rounds - 1
        if r == 0:
            for copy in arrive_l:
                copy.wait_recv()
            left_t[...] = nt(eye, lf[r].reshape(slab, width)).astype(BF16)
            gather_left()
            for copy in arrive_r:
                copy.wait_recv()
            right_t[...] = nt(eye, rf[r].reshape(slab, width)).astype(BF16)
        arrive_l, arrive_r = [], []
        whole = ne == 2 and not last
        slabs_l, slabs_r = [], []
        if whole:
            weigh(r)
            to = {"bucket": b, "edge": edge_at(1)}
            own_r[...] = nt(w_ref[...], q_ref[...]).reshape(own_r.shape)
            grs[r] = own_r[...].astype(BF16)
            slabs_r.append(send(grs.at[r], grr.at[r], sem_gr.at[r, 1], to))
            over_edges(lambda i, at: back(at, s_ref[:, at], t_ref[:, at], w_ref[:, at]))
        else:
            weigh(r, back)

        gts[r] = rel_rows(1 - core).astype(BF16)
        pairs = [send(gts.at[r, p], pair_in.at[r, p], sem_pair.at[r, p], mate) for p in range(pieces)]
        gown[...] = rel_rows(core)
        shares = [[] for _ in range(pieces)]
        for p in range(pieces):
            pairs[p].wait_recv()
            pair_sum[r, p] = (gown[p] + pair_in[r, p].astype(F32)).astype(BF16)
            for d in near:
                c, to = member(d)
                copy = remote(pair_sum.at[r, p, c], rs_in.at[r, p, slot_of(d)], sem_rs.at[r, p], to)
                copy.start()
                shares[p].append(copy)

        if whole:
            to = {"bucket": b, "edge": edge_at(1)}
            own_l[...] = (nt(hsrc[...], gs_ref[0])).reshape(own_l.shape)
            gls[r] = own_l[...].astype(BF16)
            slabs_l.append(send(gls.at[r], glr.at[r], sem_gl.at[r, 1], to))
        else:
            for d in range(1, ne):
                to = {"bucket": b, "edge": edge_at(d)}
                grs[r, d] = right_rows(edge_at(d)).astype(BF16)
                slabs_r.append(send(grs.at[r, d], grr.at[r, d], sem_gr.at[r, d], to))
            for d in range(1, ne):
                to = {"bucket": b, "edge": edge_at(d)}
                gls[r, d] = left_rows(edge_at(d)).astype(BF16)
                slabs_l.append(send(gls.at[r, d], glr.at[r, d], sem_gl.at[r, d], to))
            own_l[0] = left_rows(e)
            own_r[0] = right_rows(e)
        if not last:
            count_round(r + 1)
            mark_sources(r + 1)

        def all_but_one(ref, sems):
            return remote(ref.at[pl.ds(1, members - 1)], ref.at[pl.ds(1, members - 1)], sems, mate)

        def arrived(copies, ref, sems):
            all_but_one(ref, sems).wait_recv()

        crossed = []
        for p in range(pieces):
            arrived(shares[p], rs_in.at[r, p], sem_rs.at[r, p])
            g = gown[p, me] + pair_in[r, p, me].astype(F32)
            for d in range(1, members):
                g = g + rs_in[r, p, d].astype(F32)
            xr[r, p, 0] = g
            crossed.append([
                send(xr.at[r, p, 0], xr.at[r, p, d], sem_x.at[r, p, d], twin(d)) for d in range(1, twins)
            ])

        if not last:
            if r > 0:
                turn()
            gather_theta(r + 1)

        spread = [[] for _ in range(pieces)]
        for p in range(pieces):
            for copy in crossed[p]:
                copy.wait_recv()
            g = jnp.zeros((share, width), F32)
            for a in range(twins):
                g = g + xr[r, p, lax.rem(high + twins - a, twins)]
            ag[r, core, p, me] = g.astype(BF16)
            for d in near:
                block = ag.at[r, core, p, me]
                copy = remote(block, block, sem_ag.at[r, p], member(d)[1])
                copy.start()
                spread[p].append(copy)

        def updated(held, own, others, copies, rate):
            for copy in copies:
                copy.wait_recv()
            g = own[...] if whole else own[0]
            if whole:
                g = g + others[r].astype(F32)
                return (held[r].astype(F32) - rate * g).astype(BF16)
            for d in range(1, ne):
                g = g + others[r, d].astype(F32)
            return (held[r, e].astype(F32) - rate * g).astype(BF16)

        fresh = updated(rf, own_r, grr, slabs_r, learn_rate)
        if last:
            new_r[...] = fresh
            outs.append(pltpu.make_async_copy(new_r, right_out, sem_out.at[1]))
            outs[-1].start()
        elif whole:
            moved[r] = fresh
            to = {"bucket": ahead, "edge": e}
            arrive_r.append(send(moved.at[r], rf.at[r + 1], sem_r.at[r + 1, 0], to))
        else:
            moved[r, 0] = fresh
            for d in range(ne):
                to = {"bucket": ahead, "edge": edge_at(d)}
                arrive_r.append(send(moved.at[r, 0], rf.at[r + 1, e], sem_r.at[r + 1, d], to))
        fresh = updated(lf, own_l, glr, slabs_l, learn_rate)
        if last:
            new_l[...] = fresh
            outs.append(pltpu.make_async_copy(new_l, left_out, sem_out.at[0]))
            outs[-1].start()
        elif whole:
            lf[r + 1] = fresh
        else:
            lf[r + 1, e] = fresh
            for d in range(1, ne):
                to = {"bucket": b, "edge": edge_at(d)}
                arrive_l.append(send(lf.at[r + 1, e], lf.at[r + 1, e], sem_l.at[r + 1, d], to))
        if not last:
            for copy in arrive_l:
                copy.wait_recv()
            left_t[...] = nt(eye, lf[r + 1].reshape(slab, width)).astype(BF16)
            gather_left()

        forwards = []
        for p in range(pieces):
            arrived(spread[p], ag.at[r, core, p], sem_ag.at[r, p])
            forwards.append(send(ag.at[r, core, p], ag.at[r, core, p], sem_fw.at[r, p], mate))
        if not last:
            step_t[core] = nt(eye, ag[r, core].reshape(half, width)).astype(BF16)
            over_edges(take_step)
            for copy in arrive_r:
                copy.wait_recv()
            right_t[...] = nt(eye, rf[r + 1].reshape(slab, width)).astype(BF16)
        for h in range(2):
            where = core if h == 0 else 1 - core
            if h == 1:
                for copy in forwards:
                    copy.wait_recv()
            at = pl.ds(pl.multiple_of(where * half, half), half)
            step = ag[r, where].reshape(half, width)
            theta[at, :] = theta[at, :] - relation_rate * step.astype(F32)
            if last:
                outs.append(pltpu.make_async_copy(theta.at[at], theta_out.at[at], sem_out.at[2 + h]))
                outs[-1].start()
        if not last:
            step_t[1 - core] = nt(eye, ag[r, 1 - core].reshape(half, width)).astype(BF16)

    for copy in started:
        copy.wait_send()
    for r in range(rounds):
        for p in range(pieces):
            all_but_one(rs_in.at[r, p], sem_rs.at[r, p]).wait_send()
            all_but_one(ag.at[r, core, p], sem_ag.at[r, p]).wait_send()
    for copy in outs:
        copy.wait()


def finish(left_in, right_in, theta_in, left_out, right_out, theta_out, left, right, theta, sems):
    moves = [(left_in, left, left_out), (right_in, right, right_out)]
    part = theta.shape[0] // 4
    for i in range(4):
        at = pl.ds(i * part, part)
        moves.append((theta_in.at[at], theta.at[at], theta_out.at[at]))
    ins = [pltpu.make_async_copy(a, v, sems.at[0, i]) for i, (a, v, _) in enumerate(moves)]
    outs = [pltpu.make_async_copy(v, o, sems.at[1, i]) for i, (_, v, o) in enumerate(moves)]
    for copy in ins:
        copy.start()
    for a, o in zip(ins, outs):
        a.wait()
        o.start()
    for copy in outs:
        copy.wait()


def solution(mesh):
    nb, ne = mesh.shape["bucket"], mesh.shape["edge"]

    def body(left_slab, right_slab, relation, src_ids, dst_ids, rel_ids, neg_ids, edge_counts):
        rounds, _, blocks, negs = neg_ids.shape
        slots = src_ids.shape[2]
        span = slots // blocks
        rows, width = left_slab.shape
        slab, rels = rows * ne, relation.shape[0]
        half = rels // 2
        per = 4 if slab <= 512 else 1
        members, twins = 4 * ne, nb // 8
        pieces = max(1, min(2, half // (16 * members)))
        share = half // pieces // members
        held = ne if ne == 2 else 1
        vmem = pltpu.VMEM
        hbm = pl.BlockSpec(memory_space=pltpu.HBM)
        dma = pltpu.SemaphoreType.DMA
        cfg = (rounds, nb, ne, blocks, span, per, pieces)
        shares = (pieces, members, share, width)
        results = (
            jax.ShapeDtypeStruct((rows, width), BF16),
            jax.ShapeDtypeStruct((rows, width), BF16),
            jax.ShapeDtypeStruct((rels, width), F32),
        )
        left, right, theta = pl.pallas_call(
            functools.partial(kernel, cfg),
            out_shape=results,
            in_specs=[pl.BlockSpec(memory_space=pltpu.SMEM)] + [hbm] * 7,
            out_specs=(hbm, hbm, hbm),
            scratch_shapes=[
                vmem((rounds, 1, slots), I32),
                vmem((rounds, 1, slots), I32),
                vmem((rounds, 1, slots), I32),
                vmem((rounds, 1, blocks, negs), I32),
                vmem((rels, width), F32),
                vmem((rounds, ne, rows, width), BF16),
                vmem((rounds, ne, rows, width), BF16),
                vmem((rows, width), BF16),
                vmem((rows, width), BF16),
                vmem((rounds, blocks, slab, 128), F32),
                vmem((2 * width, rels), BF16),
                vmem((width, slab), BF16),
                vmem((width, slab), BF16),
                vmem((2, width, half), BF16),
                vmem((rels, slots), BF16),
                vmem((slab, slots), BF16),
                vmem((width, slots), F32),
                vmem((width, slots), F32),
                vmem((width, slots), BF16),
                vmem((slab, slots), BF16),
                vmem((width, slots), BF16),
                vmem((1, width, slots), BF16),
                vmem((held, rows, width), F32),
                vmem((held, rows, width), F32),
                vmem((rounds, ne, rows, width), BF16),
                vmem((rounds, ne, rows, width), BF16),
                vmem((rounds, ne, rows, width), BF16),
                vmem((rounds, ne, rows, width), BF16),
                vmem((rounds, held, rows, width), BF16),
                vmem((rounds,) + shares, BF16),
                vmem(shares, F32),
                vmem((rounds,) + shares, BF16),
                vmem((rounds,) + shares, BF16),
                vmem((rounds,) + shares, BF16),
                vmem((rounds, pieces, twins, share, width), F32),
                vmem((rounds, 2) + shares, BF16),
                dma((7,)),
                dma((4,)),
                dma((rounds, ne, 2)),
                dma((rounds, ne, 2)),
                dma((rounds, ne, 2)),
                dma((rounds, ne, 2)),
                dma((rounds, pieces, 2)),
                dma((rounds, pieces, 2)),
                dma((rounds, pieces, twins, 2)),
                dma((rounds, pieces, 2)),
                dma((rounds, pieces, 2)),
            ],
            compiler_params=pltpu.CompilerParams(
                collective_id=0, has_side_effects=True, vmem_limit_bytes=60 * 1024 * 1024
            ),
        )(edge_counts.T, left_slab, right_slab, relation, src_ids, dst_ids, rel_ids, neg_ids)
        return pl.pallas_call(
            finish,
            out_shape=results,
            in_specs=[hbm] * 3,
            out_specs=(hbm, hbm, hbm),
            scratch_shapes=[
                vmem((rows, width), BF16),
                vmem((rows, width), BF16),
                vmem((rels, width), F32),
                dma((2, 6)),
            ],
            compiler_params=pltpu.CompilerParams(vmem_limit_bytes=63 * 1024 * 1024),
        )(left, right, theta)

    placed = (
        P(("bucket", "edge"), None),
        P(("bucket", "edge"), None),
        P(),
        P(None, "bucket", "edge"),
        P(None, "bucket", "edge"),
        P(None, "bucket", "edge"),
        P(None, "bucket", "edge", None),
        P(None, "bucket"),
    )
    return jax.shard_map(
        body,
        mesh=mesh,
        in_specs=placed,
        out_specs=(P(("bucket", "edge"), None), P(("bucket", "edge"), None), P()),
        check_vma=False,
    )
```
